256 devices in a mesh: seq: 64 (over y, z, core), batch: 4 (over x).
Axes of the slice: x: 4, y: 4, z: 8, core: 2. Of those that a mesh axis runs over, the one named last changes fastest.
Arguments:
- token_ids: int32 [262144], P(('batch', 'seq')), parts along dimension 0, may hold values from 0 to 4
- embed_table: bfloat16 [5, 256], replicated, may hold values from -6 to 6
- input_weight_matrix: bfloat16 [256, 1064], replicated, may hold values from -0.375 to 0.375
- output_weight_matrix: bfloat16 [512, 256], replicated, may hold values from -0.25 to 0.25
- conv_weight: float32 [2, 4, 512], replicated, may hold values from -3 to 3
- dt_bias: float32 [2, 8], replicated, may hold values from -1 to 1
- decay_rate: float32 [2, 8], replicated, may hold values from 0 to 0.05
- skip_gain: float32 [2, 8], replicated, may hold values from -4 to 4
- norm_gain: float32 [2, 512], replicated, may hold values from 0.1 to 1.9
Outputs:
- hidden: bfloat16 [262144, 256], P(('batch', 'seq')), parts along dimension 0
The draws below stay inside these ranges and needn't reach their ends.
There are 4 independent parts, one for each index of `batch`. The reference program is written for one: setup_inputs(seed, part) draws one part's arguments, and reference() takes and returns one part's arrays. A program takes and returns all parts, laid end to end along the dimension named above; an argument that names none is the same for every part. Nothing has to cross between parts.
All inputs are finite; a program needn't handle non-finite values.
Results may differ from the reference program's by a relative error of at most 0.0029.
The reference program's roundings to bfloat16 on the way count: a program that leaves them out, or rounds other values in their place, can miss the bound.
Values may be sent and summed in bfloat16 or wider, within the bound.
A program may use at most 128 MiB of HBM per device.

```python
import math
import jax
import jax.numpy as jnp
from jax import lax

D = 256
E = 512
NS = 16
P_SIZE = 64
KW = 4
BLK = 128
L_DEV = 1024
H = 8
LENGTH = 65536


def draw_token_ids(key, part):
    span = max(L_DEV, LENGTH // 8)
    count = LENGTH // span + 2
    key_offset, key_major, key_other, key_pick = jax.random.split(key, 4)
    offset = jax.random.randint(key_offset, (), 0, span)
    stretch = (jnp.arange(LENGTH, dtype=jnp.int32) + offset) // span
    dominant = jax.random.randint(key_major, (count,), 0, 5)
    others = jax.random.randint(key_other, (LENGTH,), 0, 5)
    picked = jax.random.randint(key_pick, (LENGTH,), 0, 4) < 3
    return jnp.where(picked, dominant[stretch], others).astype(jnp.int32)


def draw_decay_rate(key, part):
    key_slow, key_fast, key_keep, key_share = jax.random.split(key, 4)
    slow_rates = jnp.exp(jax.random.uniform(key_slow, (2, H), jnp.float32, math.log(0.3), math.log(2.5))) * (1.0 / LENGTH)
    fast_rates = jnp.exp(jax.random.uniform(key_fast, (2, H), jnp.float32, math.log(0.02), math.log(0.05)))
    keeper = jax.random.randint(key_keep, (2,), 0, H)
    forced = jnp.arange(H)[None, :] == keeper[:, None]
    slow_heads = forced | (jax.random.uniform(key_share, (2, H), jnp.float32) < 0.6)
    return jnp.where(slow_heads, slow_rates, fast_rates).astype(jnp.float32)


def noise(stream_key, dims, deviation, reach, held_as=jnp.bfloat16):
    entries = deviation * jax.random.normal(stream_key, dims, jnp.float32)
    return jnp.clip(entries, min=-reach, max=reach).astype(held_as)


def setup_inputs(seed: int = 0, part: int = 0) -> dict:
    key_of = jax.random.split(jax.random.key(seed), 10)
    part_splits = jax.random.split(jax.random.fold_in(key_of[9], part), 10)
    return {
        "token_ids": draw_token_ids(jax.random.fold_in(jax.random.fold_in(key_of[9], part), 71), part),
        "embed_table": noise(key_of[1], (5, D), 1.0, 6.0),
        "input_weight_matrix": noise(key_of[2], (D, 2 * E + 2 * NS + H), D ** -0.5, 0.375),
        "output_weight_matrix": noise(key_of[3], (E, D), E ** -0.5, 0.25),
        "conv_weight": noise(key_of[4], (2, KW, E), KW ** -0.5, 3.0, jnp.float32),
        "dt_bias": jnp.clip(jax.random.uniform(key_of[5], (2, H), jnp.float32, -1.0, 1.0), -1.0, 1.0),
        "decay_rate": draw_decay_rate(jax.random.fold_in(key_of[9], 71), part),
        "skip_gain": noise(key_of[7], (2, H), 1.0, 4.0, jnp.float32),
        "norm_gain": jnp.clip(1.0 + 0.18 * jax.random.normal(key_of[8], (2, E), jnp.float32), 0.1, 1.9),
    }


EPSILON = 1e-05

def complement(ids):
    return jnp.where(ids < 4, 3 - ids, ids).astype(jnp.int32)

def embed_rows(ids, embed_table):
    onehot = (ids[:, None] == jnp.arange(5, dtype=jnp.int32)[None, :]).astype(jnp.bfloat16)
    return jnp.dot(onehot, embed_table, preferred_element_type=jnp.float32).astype(jnp.bfloat16)

def block_step(state, pieces):
    highest = lax.Precision.HIGHEST
    inner_x, log_decay, step, b_part, c_part = pieces
    count = log_decay.shape[0]
    cumul = jnp.cumsum(log_decay, axis=0)
    index = jnp.arange(count)
    lower = index[:, None] >= index[None, :]
    spread = cumul[:, None, :] - cumul[None, :, :]
    decay = jnp.exp(jnp.where(lower[:, :, None], spread, -1e+30))
    scores = jnp.dot(c_part, b_part.T, precision=highest)
    weighted = inner_x * step[:, :, None]
    inner = jnp.einsum('trh,rhp->thp', scores[:, :, None] * decay, weighted, precision=highest)
    carried = jnp.exp(cumul)[:, :, None] * jnp.einsum('tn,hpn->thp', c_part, state, precision=highest)
    tail = jnp.exp(cumul[-1][None, :] - cumul)
    new_state = jnp.exp(cumul[-1])[:, None, None] * state + jnp.einsum('rh,rhp,rn->hpn', tail, weighted, b_part, precision=highest)
    return (new_state, inner + carried)

def run_chain(inner_x, log_decay, step, b_part, c_part):
    length = log_decay.shape[0]
    blocks = length // BLK
    init = jnp.zeros((H, P_SIZE, NS), jnp.float32)
    pieces = (inner_x.reshape(blocks, BLK, H, P_SIZE), log_decay.reshape(blocks, BLK, H), step.reshape(blocks, BLK, H), b_part.reshape(blocks, BLK, NS), c_part.reshape(blocks, BLK, NS))
    _, outputs = lax.scan(block_step, init, pieces)
    return outputs.reshape(length, H, P_SIZE)

def direction(projected, k, backward, conv_weight, dt_bias, decay_rate, skip_gain, norm_gain):
    gate = projected[:, :E].astype(jnp.float32)
    values = projected[:, E:2 * E].astype(jnp.float32)
    b_part = projected[:, 2 * E:2 * E + NS].astype(jnp.float32)
    c_part = projected[:, 2 * E + NS:2 * E + 2 * NS].astype(jnp.float32)
    raw = projected[:, 2 * E + 2 * NS:].astype(jnp.float32)
    if backward:
        values, b_part, c_part, raw = (values[::-1], b_part[::-1], c_part[::-1], raw[::-1])
    length = values.shape[0]
    padded_input = jnp.concatenate([jnp.zeros((KW - 1, E), jnp.float32), values], axis=0)
    acc = conv_weight[k, 0][None, :] * padded_input[0:length]
    for j in range(1, KW):
        acc = acc + conv_weight[k, j][None, :] * padded_input[j:j + length]
    inner_x = jax.nn.silu(acc).reshape(length, H, P_SIZE)
    step = jax.nn.softplus(raw + dt_bias[k][None, :])
    log_decay = -decay_rate[k][None, :] * step
    outputs = run_chain(inner_x, log_decay, step, b_part, c_part) + skip_gain[k][None, :, None] * inner_x
    if backward:
        outputs = outputs[::-1]
    gated = outputs * jax.nn.silu(gate).reshape(length, H, P_SIZE)
    meansq = lax.optimization_barrier(jnp.mean(gated * gated, axis=-1, keepdims=True))
    normed = gated * lax.rsqrt(meansq + EPSILON) * norm_gain[k].reshape(1, H, P_SIZE)
    return normed.reshape(length, E)

def strand(feature_vectors, input_weight_matrix, output_weight_matrix, conv_weight, dt_bias, decay_rate, skip_gain, norm_gain):
    projected = jnp.dot(feature_vectors, input_weight_matrix, preferred_element_type=jnp.float32).astype(jnp.bfloat16)
    first = direction(projected, 0, False, conv_weight, dt_bias, decay_rate, skip_gain, norm_gain)
    second = direction(projected, 1, True, conv_weight, dt_bias, decay_rate, skip_gain, norm_gain)
    mixer_output = (first + second).astype(jnp.bfloat16)
    return jnp.dot(mixer_output, output_weight_matrix, preferred_element_type=jnp.float32).astype(jnp.bfloat16)

def reference(token_ids, embed_table, input_weight_matrix, output_weight_matrix, conv_weight, dt_bias, decay_rate, skip_gain, norm_gain):
    feature_vectors = embed_rows(token_ids, embed_table)
    rc_features = embed_rows(complement(token_ids[::-1]), embed_table)
    own_out = strand(feature_vectors, input_weight_matrix, output_weight_matrix, conv_weight, dt_bias, decay_rate, skip_gain, norm_gain)
    rc_out = strand(rc_features, input_weight_matrix, output_weight_matrix, conv_weight, dt_bias, decay_rate, skip_gain, norm_gain)
    hidden = feature_vectors.astype(jnp.float32) + own_out.astype(jnp.float32) + rc_out[::-1, ::-1].astype(jnp.float32)
    return hidden.astype(jnp.bfloat16)
```

```python
import functools

import jax
import jax.numpy as jnp
from jax import lax
from jax.experimental import pallas as pl
from jax.experimental.pallas import tpu as pltpu
from jax.sharding import PartitionSpec as P

D = 256
E = 512
NS = 16
KW = 4
H = 8
CH = 64
SB = 128
EPSILON = 1e-05
LOG2E = 1.4426950408889634
CHAINS = ((0, 0, False), (0, 1, True), (1, 0, True), (1, 1, False))
F32 = jnp.float32
BF16 = jnp.bfloat16


def split3(v):
    hi = v.astype(BF16)
    rest = v - hi.astype(F32)
    mid = rest.astype(BF16)
    lo = (rest - mid.astype(F32)).astype(BF16)
    return hi, mid, lo


def stack3(v):
    return jnp.concatenate(split3(v), axis=0)


def rounded(v):
    return lax.reduce_precision(v, exponent_bits=8, mantissa_bits=7)


def table3(v):
    hi = rounded(v)
    mid = rounded(v - hi)
    lo = v - hi - mid
    return jnp.concatenate([hi, mid, lo], axis=0).astype(BF16)


def dot(a, b):
    return jnp.dot(a, b, preferred_element_type=F32)


def onehots(taps_row):
    sym = lax.broadcasted_iota(jnp.int32, (8, SB), 0)
    return [(taps_row[j : j + 1, :] == sym).astype(F32) for j in range(8)]


def counts(center, backward):
    r = lax.broadcasted_iota(jnp.int32, (SB, SB), 0)
    c = lax.broadcasted_iota(jnp.int32, (SB, SB), 1)
    same = (r // CH) == (c // CH)
    keep = same & ((c >= r) if backward else (c <= r))
    return dot(keep.astype(BF16), center).astype(BF16)


def local_kernel(taps_ref, ct_ref, la_ref, dt_ref, s_ref, skip_ref, y_ref, u_ref, end_ref, dacc_ref, eacc_ref):
    step = pl.program_id(0)

    @pl.when(step == 0)
    def _():
        dacc_ref[...] = jnp.zeros_like(dacc_ref)
        eacc_ref[...] = jnp.zeros_like(eacc_ref)

    oht = onehots(taps_ref[...])
    oh = jnp.concatenate(oht, axis=0).T.astype(BF16)
    center = jnp.concatenate([oht[3]] * 16, axis=0).T.astype(BF16)
    center = center[:, :24]
    oh192 = jnp.concatenate([oh, oh, oh], axis=1)
    cnt = (counts(center, False), counts(center, True))

    lane = lax.broadcasted_iota(jnp.int32, (CH, SB), 1)
    row = lax.broadcasted_iota(jnp.int32, (CH, SB), 0)
    within = lane % CH
    diag = within == row
    low = lane < CH
    neg = (
        jnp.where(within <= row, 0.0, -1e30).astype(F32),
        jnp.where(within >= row, 0.0, -1e30).astype(F32),
    )
    lane8 = lax.broadcasted_iota(jnp.int32, (8, SB), 1)
    row8 = lax.broadcasted_iota(jnp.int32, (8, SB), 0)
    rolled = pltpu.roll(oht[3], CH, 1)
    ot2 = (jnp.where(lane8 < CH, oht[3], rolled), jnp.where(lane8 < CH, rolled, oht[3]))

    scores = []
    for strand in range(2):
        per_chunk = []
        for c in range(2):
            acc = None
            for b in range(5):
                term = s_ref[strand, b] * ot2[c][b : b + 1, :]
                acc = term if acc is None else acc + term
            per_chunk.append(dot(center[c * CH : (c + 1) * CH], stack3(acc)))
        scores.append(per_chunk)

    for n, (strand, k, backward) in enumerate(CHAINS):
        d = int(backward)
        for pair in range(4):
            cols = slice(n * E + pair * SB, n * E + (pair + 1) * SB)
            pre = dot(oh192, ct_ref[:, cols])
            xc = pre * jax.nn.sigmoid(pre)
            xw = xc * dot(center, dt_ref[:, cols])
            cum = dot(cnt[d], la_ref[:, cols])
            xh = xw.astype(BF16)
            xl = (xw - xh.astype(F32)).astype(BF16)
            for c in range(2):
                rows = slice(c * CH, (c + 1) * CH)
                cc = cum[rows]
                rowv = jnp.sum(jnp.where(diag, cc, 0.0), axis=0, keepdims=True)
                last = cc[0:1, :] if backward else cc[CH - 1 : CH, :]
                m = jnp.exp2(jnp.minimum(cc - rowv, neg[d])) * scores[strand][c]
                ext = jnp.exp2(jnp.minimum(last - rowv, 0.0)) * ot2[c]
                full = jnp.concatenate([m, ext, jnp.zeros_like(ext)], axis=0)
                mh = full.astype(BF16)
                ml = (full - mh.astype(F32)).astype(BF16)
                lhs = jnp.concatenate([mh, ml], axis=1)
                zero = jnp.zeros((CH, SB), BF16)
                top = jnp.concatenate([jnp.where(low, xh[rows], zero), jnp.where(low, xl[rows], zero)], axis=1)
                bot = jnp.concatenate([jnp.where(low, zero, xh[rows]), jnp.where(low, zero, xl[rows])], axis=1)
                rhs = jnp.concatenate([top, bot, top, bot], axis=0)
                out = dot(lhs, rhs)
                out = out[:, :SB] + out[:, SB:]
                y_ref[rows, cols] = out[:CH] + skip_ref[0:1, cols] * xc[rows]
                u = out[CH : CH + 8]
                ps = slice(pair * SB, (pair + 1) * SB)
                u_ref[c, n, :, ps] = jnp.where(row8 == 5, jnp.broadcast_to(last, (8, SB)), u)
                dacc = dacc_ref[n, 0:1, ps]
                eacc = eacc_ref[n, :, ps]
                if backward:
                    eacc = eacc + jnp.exp2(dacc) * u
                else:
                    eacc = eacc * jnp.exp2(last) + u
                dacc = dacc + last
                dacc_ref[n, 0:1, ps] = dacc
                eacc_ref[n, :, ps] = eacc
                end_ref[n, :, ps] = jnp.where(row8 == 5, jnp.broadcast_to(dacc, (8, SB)), eacc)


def finish_kernel(
    count, chunks, me_ref, taps_ref, la_ref, s_ref, gate_ref, gain_ref, emb_ref, wo_ref, u_ref, all_ref, y_ref,
    out_ref, in_ref
):
    step = pl.program_id(0)

    @pl.when(step == 0)
    def _():
        me = me_ref[0]
        for n, (strand, k, backward) in enumerate(CHAINS):

            def hop(i, s):
                j = count - 1 - i if backward else i
                piece = all_ref[j, n]
                use = (j > me) if backward else (j < me)
                return jnp.where(use, jnp.exp2(piece[5:6, :]) * s + piece, s)

            s = lax.fori_loop(0, count, hop, jnp.zeros((8, E), F32))

            def chunk(i, s):
                c = chunks - 1 - i if backward else i
                acc = None
                for b in range(5):
                    col = s_ref[strand, b]
                    term = jnp.concatenate([col] * 4, axis=1) * s[b : b + 1, :]
                    acc = term if acc is None else acc + term
                hi, mid, lo = split3(acc)
                in_ref[c, n] = jnp.concatenate(
                    [hi.astype(F32), mid.astype(F32), lo.astype(F32)], axis=0
                )
                piece = u_ref[c, n]
                return jnp.exp2(piece[5:6, :]) * s + piece

            lax.fori_loop(0, chunks, chunk, s)

    center = (
        taps_ref[3:4, :] == lax.broadcasted_iota(jnp.int32, (SB, SB), 0) % 8
    ).astype(F32).T.astype(BF16)[:, :24]
    cnt = (counts(center, False), counts(center, True))
    r = lax.broadcasted_iota(jnp.int32, (2 * SB, SB), 0)
    c = lax.broadcasted_iota(jnp.int32, (2 * SB, SB), 1)
    ones = (((r % SB) // CH) == (c // CH)).astype(BF16)

    total = dot(center[:, :8], emb_ref[...])
    for strand in range(2):
        mixed = []
        for pair in range(4):
            gate = dot(center, gate_ref[:, strand * E + pair * SB : strand * E + (pair + 1) * SB])
            ps = slice(pair * SB, (pair + 1) * SB)
            acc = None
            for k in range(2):
                n = strand * 2 + k
                backward = CHAINS[n][2]
                cols = slice(n * E + pair * SB, n * E + (pair + 1) * SB)
                reach = jnp.exp2(dot(cnt[int(backward)], la_ref[:, cols]))
                far = jnp.concatenate(
                    [
                        dot(center[h * CH : (h + 1) * CH], in_ref[step * 2 + h, n, :, ps].astype(BF16))
                        for h in range(2)
                    ],
                    axis=0,
                )
                g = (y_ref[:, cols] + reach * far) * gate
                sq = g * g
                sh = sq.astype(BF16)
                sl = (sq - sh.astype(F32)).astype(BF16)
                mean = dot(jnp.concatenate([sh, sl], axis=1), ones) * (1.0 / CH)
                normed = g * lax.rsqrt(mean + EPSILON) * gain_ref[k : k + 1, ps]
                acc = normed if acc is None else acc + normed
            mixed.append(acc.astype(BF16))
        strand_out = dot(jnp.concatenate(mixed, axis=1), wo_ref[strand])
        total = total + strand_out.astype(BF16).astype(F32)
    out_ref[...] = total.astype(BF16)


def per_device(
    token_ids,
    embed_table,
    input_weight_matrix,
    output_weight_matrix,
    conv_weight,
    dt_bias,
    decay_rate,
    skip_gain,
    norm_gain,
):
    rows = token_ids.shape[0]
    count = lax.axis_size("seq")
    blocks = rows // SB
    chunks = rows // CH
    rim = KW - 1

    edge = token_ids + 1
    left = lax.ppermute(edge[rows - rim :], "seq", [(i, i + 1) for i in range(count - 1)]) - 1
    right = lax.ppermute(edge[:rim], "seq", [(i + 1, i) for i in range(count - 1)]) - 1
    ext = jnp.concatenate([left, token_ids, right])
    taps = jnp.stack([ext[j : j + rows] for j in range(2 * rim + 1)] + [jnp.full((rows,), -1, jnp.int32)])

    both = jnp.stack([embed_table, embed_table[jnp.array([3, 2, 1, 0, 4])]])
    table = jnp.einsum("sad,df->saf", both, input_weight_matrix, preferred_element_type=F32)
    table = jnp.pad(rounded(table), ((0, 0), (0, 3), (0, 0)))
    gate = table[:, :, :E]
    values = table[:, :, E : 2 * E]
    b_part = table[:, :, 2 * E : 2 * E + NS]
    c_part = table[:, :, 2 * E + NS : 2 * E + 2 * NS]
    raw = table[:, :, 2 * E + 2 * NS :]

    conv_rows, dts, las = [], [], []
    for strand, k, backward in CHAINS:
        zero = jnp.zeros((8, E), F32)
        parts = []
        for j in range(8):
            tap = (2 * rim - j) if backward else j
            parts.append(conv_weight[k, tap][None, :] * values[strand] if 0 <= tap < KW else zero)
        conv_rows.append(jnp.concatenate(parts, axis=0))
        dt = jax.nn.softplus(raw[strand] + dt_bias[k][None, :])
        dts.append(jnp.repeat(dt, CH, axis=1))
        las.append(jnp.repeat(-decay_rate[k][None, :] * dt * LOG2E, CH, axis=1))
    ct = table3(jnp.concatenate(conv_rows, axis=1))
    dt3 = table3(jnp.concatenate(dts, axis=1))
    la3 = table3(jnp.concatenate(las, axis=1))
    gate3 = table3(jnp.concatenate(list(gate * jax.nn.sigmoid(gate)), axis=1))
    skip = jnp.concatenate([jnp.repeat(skip_gain[k], CH) for _, k, _ in CHAINS])[None, :]
    score = jnp.sum(c_part[:, :, None, :] * b_part[:, None, :, :], axis=-1)
    valid = (jnp.arange(8) < 5).astype(F32)
    score = score * valid[None, :, None] * valid[None, None, :]
    score = jnp.broadcast_to(jnp.swapaxes(score, 1, 2)[:, :, :, None], (2, 8, 8, SB))
    emb8 = jnp.pad(embed_table, ((0, 3), (0, 0)))
    wo = jnp.stack([output_weight_matrix, output_weight_matrix[:, ::-1]])

    whole = lambda shape: pl.BlockSpec(shape, lambda i: (0,) * len(shape))
    params = pltpu.CompilerParams(vmem_limit_bytes=56 * 1024 * 1024)
    y, u, end = pl.pallas_call(
        local_kernel,
        grid=(blocks,),
        out_shape=(
            jax.ShapeDtypeStruct((rows, 4 * E), F32),
            jax.ShapeDtypeStruct((chunks, 4, 8, E), F32),
            jax.ShapeDtypeStruct((4, 8, E), F32),
        ),
        in_specs=[
            pl.BlockSpec((8, SB), lambda i: (0, i)),
            whole((192, 4 * E)),
            whole((24, 4 * E)),
            whole((24, 4 * E)),
            whole((2, 8, 8, SB)),
            whole((1, 4 * E)),
        ],
        out_specs=(
            pl.BlockSpec((SB, 4 * E), lambda i: (i, 0)),
            pl.BlockSpec((2, 4, 8, E), lambda i: (i, 0, 0, 0)),
            whole((4, 8, E)),
        ),
        scratch_shapes=[pltpu.VMEM((4, 8, E), F32), pltpu.VMEM((4, 8, E), F32)],
        compiler_params=params,
        name="local_chunks",
    )(taps, ct, la3, dt3, score, skip)

    gathered = lax.all_gather(end, "seq")
    me = lax.axis_index("seq").astype(jnp.int32).reshape(1)
    return pl.pallas_call(
        functools.partial(finish_kernel, count, chunks),
        grid=(blocks,),
        out_shape=jax.ShapeDtypeStruct((rows, D), BF16),
        in_specs=[
            pl.BlockSpec(memory_space=pltpu.SMEM),
            pl.BlockSpec((8, SB), lambda i: (0, i)),
            whole((24, 4 * E)),
            whole((2, 8, 8, SB)),
            whole((24, 2 * E)),
            whole((2, E)),
            whole((8, D)),
            whole((2, E, D)),
            whole((chunks, 4, 8, E)),
            whole((count, 4, 8, E)),
            pl.BlockSpec((SB, 4 * E), lambda i: (i, 0)),
        ],
        out_specs=pl.BlockSpec((SB, D), lambda i: (i, 0)),
        scratch_shapes=[pltpu.VMEM((chunks, 4, 24, E), F32)],
        compiler_params=params,
        name="finish_rows",
    )(me, taps, la3, score, gate3, norm_gain, emb8, wo, u, gathered, y)


def solution(mesh):
    placed = (P(("batch", "seq")), P(), P(), P(), P(), P(), P(), P(), P())
    return jax.shard_map(
        per_device, mesh=mesh, in_specs=placed, out_specs=P(("batch", "seq"), None), check_vma=False
    )
```

```python
import functools

import jax
import jax.numpy as jnp
from jax import lax
from jax.experimental import pallas as pl
from jax.experimental.pallas import tpu as pltpu
from jax.sharding import PartitionSpec as P

D = 256
E = 512
NS = 16
KW = 4
H = 8
CH = 64
SB = 128
EPSILON = 1e-05
LOG2E = 1.4426950408889634
CORES = 2
NZ = 8
CHAINS = ((0, 0, False), (1, 1, False), (0, 1, True), (1, 0, True))
MESH = pl.DeviceIdType.MESH
F32 = jnp.float32
BF16 = jnp.bfloat16


def split3(v):
    hi = v.astype(BF16)
    rest = v - hi.astype(F32)
    mid = rest.astype(BF16)
    lo = (rest - mid.astype(F32)).astype(BF16)
    return hi, mid, lo


def stack3(v):
    return jnp.concatenate(split3(v), axis=0)


def dot(a, b):
    return jnp.dot(a, b, preferred_element_type=F32)


def onehots(taps_row):
    sym = lax.broadcasted_iota(jnp.int32, (8, SB), 0)
    return [(taps_row[j : j + 1, :] == sym).astype(F32) for j in range(8)]


def counts(center, backward):
    r = lax.broadcasted_iota(jnp.int32, (SB, SB), 0)
    c = lax.broadcasted_iota(jnp.int32, (SB, SB), 1)
    same = (r // CH) == (c // CH)
    keep = same & ((c >= r) if backward else (c <= r))
    return dot(keep.astype(BF16), center).astype(BF16)


def local_kernel(taps_ref, ct_ref, la_ref, dt_ref, s_ref, skip_ref, y_ref, u_ref, end_ref, dacc_ref, eacc_ref):
    step = pl.program_id(0)

    @pl.when(step == 0)
    def _():
        dacc_ref[...] = jnp.zeros_like(dacc_ref)
        eacc_ref[...] = jnp.zeros_like(eacc_ref)

    oht = onehots(taps_ref[...])
    oh = jnp.concatenate(oht, axis=0).T.astype(BF16)
    center = jnp.concatenate([oht[3]] * 16, axis=0).T.astype(BF16)
    center = center[:, :24]
    oh192 = jnp.concatenate([oh, oh, oh], axis=1)
    cnt = (counts(center, False), counts(center, True))

    lane = lax.broadcasted_iota(jnp.int32, (CH, SB), 1)
    row = lax.broadcasted_iota(jnp.int32, (CH, SB), 0)
    within = lane % CH
    diag = within == row
    low = lane < CH
    neg = (
        jnp.where(within <= row, 0.0, -1e30).astype(F32),
        jnp.where(within >= row, 0.0, -1e30).astype(F32),
    )
    lane8 = lax.broadcasted_iota(jnp.int32, (8, SB), 1)
    row8 = lax.broadcasted_iota(jnp.int32, (8, SB), 0)
    rolled = pltpu.roll(oht[3], CH, 1)
    ot2 = (jnp.where(lane8 < CH, oht[3], rolled), jnp.where(lane8 < CH, rolled, oht[3]))

    scores = []
    for strand in range(2):
        per_chunk = []
        for c in range(2):
            acc = None
            for b in range(5):
                term = s_ref[strand, b] * ot2[c][b : b + 1, :]
                acc = term if acc is None else acc + term
            per_chunk.append(dot(center[c * CH : (c + 1) * CH], stack3(acc)))
        scores.append(per_chunk)

    for n, (strand, k, backward) in enumerate(CHAINS):
        d = int(backward)
        for pair in range(4):
            cols = slice(n * E + pair * SB, n * E + (pair + 1) * SB)
            pre = dot(oh192, ct_ref[:, cols])
            xc = pre * jax.nn.sigmoid(pre)
            xw = xc * dot(center, dt_ref[:, cols])
            cum = dot(cnt[d], la_ref[:, cols])
            xh = xw.astype(BF16)
            xl = (xw - xh.astype(F32)).astype(BF16)
            for c in range(2):
                rows = slice(c * CH, (c + 1) * CH)
                cc = cum[rows]
                rowv = jnp.sum(jnp.where(diag, cc, 0.0), axis=0, keepdims=True)
                last = cc[0:1, :] if backward else cc[CH - 1 : CH, :]
                m = jnp.exp2(jnp.minimum(cc - rowv, neg[d])) * scores[strand][c]
                ext = jnp.exp2(jnp.minimum(last - rowv, 0.0)) * ot2[c]
                full = jnp.concatenate([m, ext, jnp.zeros_like(ext)], axis=0)
                mh = full.astype(BF16)
                ml = (full - mh.astype(F32)).astype(BF16)
                lhs = jnp.concatenate([mh, ml], axis=1)
                zero = jnp.zeros((CH, SB), BF16)
                top = jnp.concatenate([jnp.where(low, xh[rows], zero), jnp.where(low, xl[rows], zero)], axis=1)
                bot = jnp.concatenate([jnp.where(low, zero, xh[rows]), jnp.where(low, zero, xl[rows])], axis=1)
                rhs = jnp.concatenate([top, bot, top, bot], axis=0)
                out = dot(lhs, rhs)
                out = out[:, :SB] + out[:, SB:]
                y_ref[rows, cols] = out[:CH] + skip_ref[0:1, cols] * xc[rows]
                u = out[CH : CH + 8]
                ps = slice(pair * SB, (pair + 1) * SB)
                u_ref[c, n, :, ps] = jnp.where(row8 == 5, jnp.broadcast_to(last, (8, SB)), u)
                dacc = dacc_ref[n, 0:1, ps]
                eacc = eacc_ref[n, :, ps]
                if backward:
                    eacc = eacc + jnp.exp2(dacc) * u
                else:
                    eacc = eacc * jnp.exp2(last) + u
                dacc = dacc + last
                dacc_ref[n, 0:1, ps] = dacc
                eacc_ref[n, :, ps] = eacc
                end_ref[n, :, ps] = jnp.where(row8 == 5, jnp.broadcast_to(dacc, (8, SB)), eacc)


def finish_kernel(
    chunks, taps_ref, la_ref, s_ref, gate_ref, gain_ref, emb_ref, wo_ref, u_ref, far_ref, y_ref, out_ref, in_ref
):
    step = pl.program_id(0)

    @pl.when(step == 0)
    def _():
        for n, (strand, k, backward) in enumerate(CHAINS):

            def chunk(i, s):
                c = chunks - 1 - i if backward else i
                acc = None
                for b in range(5):
                    col = s_ref[strand, b]
                    term = jnp.concatenate([col] * 4, axis=1) * s[b : b + 1, :]
                    acc = term if acc is None else acc + term
                hi, mid, lo = split3(acc)
                in_ref[c, n] = jnp.concatenate(
                    [hi.astype(F32), mid.astype(F32), lo.astype(F32)], axis=0
                )
                piece = u_ref[c, n]
                return jnp.exp2(piece[5:6, :]) * s + piece

            lax.fori_loop(0, chunks, chunk, far_ref[int(backward), (n % 2) * 8 : (n % 2) * 8 + 8, :])

    center = (
        taps_ref[3:4, :] == lax.broadcasted_iota(jnp.int32, (SB, SB), 0) % 8
    ).astype(F32).T.astype(BF16)[:, :24]
    cnt = (counts(center, False), counts(center, True))
    r = lax.broadcasted_iota(jnp.int32, (2 * SB, SB), 0)
    c = lax.broadcasted_iota(jnp.int32, (2 * SB, SB), 1)
    ones = (((r % SB) // CH) == (c // CH)).astype(BF16)

    total = dot(center[:, :8], emb_ref[...])
    for strand in range(2):
        mixed = []
        for pair in range(4):
            gate = dot(center, gate_ref[:, strand * E + pair * SB : strand * E + (pair + 1) * SB])
            ps = slice(pair * SB, (pair + 1) * SB)
            acc = None
            for k in range(2):
                n = [c[:2] for c in CHAINS].index((strand, k))
                backward = CHAINS[n][2]
                cols = slice(n * E + pair * SB, n * E + (pair + 1) * SB)
                reach = jnp.exp2(dot(cnt[int(backward)], la_ref[:, cols]))
                far = jnp.concatenate(
                    [
                        dot(center[h * CH : (h + 1) * CH], in_ref[step * 2 + h, n, :, ps].astype(BF16))
                        for h in range(2)
                    ],
                    axis=0,
                )
                g = (y_ref[:, cols] + reach * far) * gate
                sq = g * g
                sh = sq.astype(BF16)
                sl = (sq - sh.astype(F32)).astype(BF16)
                mean = dot(jnp.concatenate([sh, sl], axis=1), ones) * (1.0 / CH)
                normed = g * lax.rsqrt(mean + EPSILON) * gain_ref[k : k + 1, ps]
                acc = normed if acc is None else acc + normed
            mixed.append(acc.astype(BF16))
        strand_out = dot(jnp.concatenate(mixed, axis=1), wo_ref[strand])
        total = total + strand_out.astype(BF16).astype(F32)
    out_ref[...] = total.astype(BF16)


def greet(peers):
    barrier = pltpu.get_barrier_semaphore()
    for peer in peers:
        pl.semaphore_signal(barrier, inc=1, device_id={"seq": peer}, device_id_type=MESH)
    pl.semaphore_wait(barrier, len(peers))


def tables_kernel(
    count, tok_ref, emb_ref, w_ref, conv_ref, hp_ref, ct_ref, la_ref, dt_ref, gate_ref, s_ref, left_ref, right_ref,
    halo_ref, send_sem, recv_sem
):
    me = lax.axis_index("seq")
    up, down = lax.rem(me + 1, count), lax.rem(me + count - 1, count)
    greet((up, down))
    copies = [
        pltpu.make_async_remote_copy(
            src_ref=tok_ref.at[src], dst_ref=halo_ref.at[slot], send_sem=send_sem.at[slot],
            recv_sem=recv_sem.at[slot], device_id={"seq": peer}, device_id_type=MESH,
        )
        for slot, src, peer in ((0, tok_ref.shape[0] - 1, up), (1, 0, down))
    ]
    for copy in copies:
        copy.start()

    sym = lax.broadcasted_iota(jnp.int32, (16, 5), 0)
    col = lax.broadcasted_iota(jnp.int32, (16, 5), 1)
    paired = jnp.where(sym < 8, sym, jnp.where(sym < 12, 11 - sym, sym - 8))
    both = dot((paired == col).astype(BF16), emb_ref[...]).astype(BF16)
    table = dot(both, w_ref[...]).astype(BF16)
    gate = table[:, :E].astype(F32)
    gate = gate * jax.nn.sigmoid(gate)
    values = table[:, E : 2 * E].astype(F32)
    tail = table[:, 2 * E :]
    width = tail.shape[1]

    def pick(first, cols, group):
        r = lax.broadcasted_iota(jnp.int32, (width, cols), 0)
        c = lax.broadcasted_iota(jnp.int32, (width, cols), 1)
        return dot(tail, (r - first == c // group).astype(BF16))

    raw = pick(2 * NS, E, CH)
    b_part, c_part = pick(0, NS, 1), pick(NS, NS, 1)
    for strand in range(2):
        at = slice(strand * 8, strand * 8 + 8)
        gate_ref[:, strand * E : (strand + 1) * E] = stack3(gate[at])
        for b in range(8):
            row = b_part[strand * 8 + b : strand * 8 + b + 1, :]
            s_ref[strand, b] = jnp.broadcast_to(jnp.sum(c_part[at] * row, axis=1, keepdims=True), (8, SB))
    for n, (strand, k, backward) in enumerate(CHAINS):
        at = slice(strand * 8, strand * 8 + 8)
        cols = slice(n * E, (n + 1) * E)
        zero = jnp.zeros((8, E), F32)
        parts = []
        for j in range(8):
            tap = (2 * (KW - 1) - j) if backward else j
            parts.append(conv_ref[k, tap : tap + 1, :] * values[at] if 0 <= tap < KW else zero)
        ct_ref[:, cols] = stack3(jnp.concatenate(parts, axis=0))
        dt = jax.nn.softplus(raw[at] + hp_ref[k : k + 1, :])
        dt_ref[:, cols] = stack3(dt)
        la_ref[:, cols] = stack3(-hp_ref[2 + k : 3 + k, :] * dt * LOG2E)

    for copy in copies:
        copy.wait()
    left_ref[...] = halo_ref[0]
    right_ref[...] = halo_ref[1]


def compose(earlier, later):
    row = lax.broadcasted_iota(jnp.int32, (8, E), 0)
    parts = []
    for i in range(2):
        e, l = earlier[8 * i : 8 * i + 8], later[8 * i : 8 * i + 8]
        parts.append(jnp.where(row == 5, 1.0, jnp.exp2(l[5:6, :])) * e + l)
    return jnp.concatenate(parts, axis=0)


def scan_kernel(
    count, end_ref, in_ref, pair_ref, back_ref, chip_ref, z_ref, line_ref, y_ref, other_ref, send_sem, recv_sem,
    zsend_sem, zrecv_sem, ysend_sem, yrecv_sem
):
    nz, ny = NZ, count // (NZ * CORES)
    me = lax.axis_index("seq")
    core = lax.rem(me, CORES)
    z = lax.rem(me // CORES, nz)
    y = me // (CORES * nz)
    sign = 1 - 2 * core
    pz = z * sign + core * (nz - 1)
    py = y * sign + core * (ny - 1)
    partner = me + sign
    zpeers = [(y * nz + lax.rem(z + d * sign + nz, nz)) * CORES + core for d in range(1, nz)]
    ypeers = [(lax.rem(y + d * sign + ny, ny) * nz + z) * CORES + core for d in range(1, ny)]
    greet([partner] + zpeers + ypeers)

    def remote(src, dst, send, recv, peer):
        return pltpu.make_async_remote_copy(
            src_ref=src, dst_ref=dst, send_sem=send, recv_sem=recv, device_id={"seq": peer}, device_id_type=MESH
        )

    def merge(position, size, slots_ref, mine):
        before = jnp.zeros_like(mine)
        for d in range(size - 1, 0, -1):
            before = jnp.where(d <= position, compose(before, slots_ref[d - 1]), before)
        total = compose(before, mine)
        for d in range(size - 1, 0, -1):
            total = jnp.where(d > position, compose(total, slots_ref[d - 1]), total)
        return before, total

    copy = remote(end_ref.at[1 - core], pair_ref, send_sem.at[0], recv_sem.at[0], partner)
    copy.start()
    copy.wait()
    mine = end_ref[core]
    chip = compose(mine, pair_ref[...])
    chip_ref[...] = chip
    copies = [
        remote(chip_ref, z_ref.at[d], zsend_sem.at[d], zrecv_sem.at[d], peer) for d, peer in enumerate(zpeers)
    ]
    for copy in copies:
        copy.start()
    for copy in copies:
        copy.wait()
    before, line = merge(pz, nz, z_ref, chip)
    line_ref[...] = line
    copies = [
        remote(line_ref, y_ref.at[d], ysend_sem.at[d], yrecv_sem.at[d], peer) for d, peer in enumerate(ypeers)
    ]
    for copy in copies:
        copy.start()
    for copy in copies:
        copy.wait()
    far, _ = merge(py, ny, y_ref, line)
    incoming = compose(far, before)
    other_ref[...] = compose(incoming, mine)
    copy = remote(other_ref, back_ref, send_sem.at[1], recv_sem.at[1], partner)
    copy.start()
    copy.wait()
    in_ref[core] = incoming
    in_ref[1 - core] = back_ref[...]


def per_device(
    token_ids,
    embed_table,
    input_weight_matrix,
    output_weight_matrix,
    conv_weight,
    dt_bias,
    decay_rate,
    skip_gain,
    norm_gain,
):
    rows = token_ids.shape[0]
    count = lax.axis_size("seq")
    blocks = rows // SB
    chunks = rows // CH
    rim = KW - 1

    hp = jnp.concatenate([jnp.repeat(v, CH, axis=1) for v in (dt_bias, decay_rate, skip_gain)])
    skip = jnp.concatenate([hp[4 + k] for _, k, _ in CHAINS])[None, :]
    emb8 = jnp.pad(embed_table, ((0, 3), (0, 0)))
    wo = jnp.stack([output_weight_matrix, output_weight_matrix[:, ::-1]])
    vmem = pl.BlockSpec(memory_space=pltpu.VMEM)

    token_rows = token_ids.reshape(rows // SB, 1, SB)
    ct, la3, dt3, gate3, score, left, right = pl.pallas_call(
        functools.partial(tables_kernel, count),
        out_shape=(
            jax.ShapeDtypeStruct((192, 4 * E), BF16),
            jax.ShapeDtypeStruct((24, 4 * E), BF16),
            jax.ShapeDtypeStruct((24, 4 * E), BF16),
            jax.ShapeDtypeStruct((24, 2 * E), BF16),
            jax.ShapeDtypeStruct((2, 8, 8, SB), F32),
            jax.ShapeDtypeStruct((1, SB), jnp.int32),
            jax.ShapeDtypeStruct((1, SB), jnp.int32),
        ),
        in_specs=[vmem] * 5,
        out_specs=(vmem,) * 7,
        scratch_shapes=[
            pltpu.VMEM((2, 1, SB), jnp.int32), pltpu.SemaphoreType.DMA((2,)), pltpu.SemaphoreType.DMA((2,))
        ],
        compiler_params=pltpu.CompilerParams(collective_id=0, has_side_effects=True),
        name="tables",
    )(token_rows, embed_table, input_weight_matrix, conv_weight, hp)
    me = lax.axis_index("seq")
    left = jnp.where(me > 0, left[0, SB - rim :], -1)
    right = jnp.where(me < count - 1, right[0, :rim], -1)
    ext = jnp.concatenate([left, token_ids, right])
    taps = jnp.stack([ext[j : j + rows] for j in range(2 * rim + 1)] + [jnp.full((rows,), -1, jnp.int32)])

    whole = lambda shape: pl.BlockSpec(shape, lambda i: (0,) * len(shape))
    params = pltpu.CompilerParams(vmem_limit_bytes=56 * 1024 * 1024)
    y, u, end = pl.pallas_call(
        local_kernel,
        grid=(blocks,),
        out_shape=(
            jax.ShapeDtypeStruct((rows, 4 * E), F32),
            jax.ShapeDtypeStruct((chunks, 4, 8, E), F32),
            jax.ShapeDtypeStruct((4, 8, E), F32),
        ),
        in_specs=[
            pl.BlockSpec((8, SB), lambda i: (0, i)),
            whole((192, 4 * E)),
            whole((24, 4 * E)),
            whole((24, 4 * E)),
            whole((2, 8, 8, SB)),
            whole((1, 4 * E)),
        ],
        out_specs=(
            pl.BlockSpec((SB, 4 * E), lambda i: (i, 0)),
            pl.BlockSpec((2, 4, 8, E), lambda i: (i, 0, 0, 0)),
            whole((4, 8, E)),
        ),
        scratch_shapes=[pltpu.VMEM((4, 8, E), F32), pltpu.VMEM((4, 8, E), F32)],
        compiler_params=params,
        name="local_chunks",
    )(taps, ct, la3, dt3, score, skip)

    nz, ny = NZ, count // (NZ * CORES)
    state = pltpu.VMEM((16, E), F32)
    far = pl.pallas_call(
        functools.partial(scan_kernel, count),
        out_shape=jax.ShapeDtypeStruct((2, 16, E), F32),
        in_specs=[vmem],
        out_specs=vmem,
        scratch_shapes=[
            state,
            state,
            state,
            pltpu.VMEM((max(nz - 1, 1), 16, E), F32),
            state,
            pltpu.VMEM((max(ny - 1, 1), 16, E), F32),
            state,
        ]
        + [pltpu.SemaphoreType.DMA((max(m, 1),)) for m in (2, 2, nz - 1, nz - 1, ny - 1, ny - 1)],
        compiler_params=pltpu.CompilerParams(collective_id=1, has_side_effects=True),
        name="state_scan",
    )(end.reshape(2, 16, E))
    return pl.pallas_call(
        functools.partial(finish_kernel, chunks),
        grid=(blocks,),
        out_shape=jax.ShapeDtypeStruct((rows, D), BF16),
        in_specs=[
            pl.BlockSpec((8, SB), lambda i: (0, i)),
            whole((24, 4 * E)),
            whole((2, 8, 8, SB)),
            whole((24, 2 * E)),
            whole((2, E)),
            whole((8, D)),
            whole((2, E, D)),
            whole((chunks, 4, 8, E)),
            whole((2, 16, E)),
            pl.BlockSpec((SB, 4 * E), lambda i: (i, 0)),
        ],
        out_specs=pl.BlockSpec((SB, D), lambda i: (i, 0)),
        scratch_shapes=[pltpu.VMEM((chunks, 4, 24, E), F32)],
        compiler_params=params,
        name="finish_rows",
    )(taps, la3, score, gate3, norm_gain, emb8, wo, u, far, y)


def solution(mesh):
    placed = (P(("batch", "seq")), P(), P(), P(), P(), P(), P(), P(), P())
    return jax.shard_map(
        per_device, mesh=mesh, in_specs=placed, out_specs=P(("batch", "seq"), None), check_vma=False
    )
```

```python
import functools

import jax
import jax.numpy as jnp
from jax import lax
from jax.experimental import pallas as pl
from jax.experimental.pallas import tpu as pltpu
from jax.sharding import PartitionSpec as P

D = 256
E = 512
NS = 16
KW = 4
H = 8
CH = 64
SB = 128
EPSILON = 1e-05
LOG2E = 1.4426950408889634
CORES = 2
NZ = 8
CHAINS = ((0, 0, False), (1, 1, False), (0, 1, True), (1, 0, True))
MESH = pl.DeviceIdType.MESH
F32 = jnp.float32
BF16 = jnp.bfloat16


def split3(v):
    hi = v.astype(BF16)
    rest = v - hi.astype(F32)
    mid = rest.astype(BF16)
    lo = (rest - mid.astype(F32)).astype(BF16)
    return hi, mid, lo


def stack3(v):
    return jnp.concatenate(split3(v), axis=0)


def dot(a, b):
    return jnp.dot(a, b, preferred_element_type=F32)


def onehots(taps_row):
    sym = lax.broadcasted_iota(jnp.int32, (8, SB), 0)
    return [(taps_row[j : j + 1, :] == sym).astype(F32) for j in range(8)]


def counts(center, backward):
    r = lax.broadcasted_iota(jnp.int32, (SB, SB), 0)
    c = lax.broadcasted_iota(jnp.int32, (SB, SB), 1)
    same = (r // CH) == (c // CH)
    keep = same & ((c >= r) if backward else (c <= r))
    return dot(keep.astype(BF16), center).astype(BF16)


def local_kernel(taps_ref, tab_ref, s_ref, skip_ref, y_ref, u_ref, end_ref, dacc_ref, eacc_ref):
    step = pl.program_id(0)

    @pl.when(step == 0)
    def _():
        dacc_ref[...] = jnp.zeros_like(dacc_ref)
        eacc_ref[...] = jnp.zeros_like(eacc_ref)

    oht = onehots(taps_ref[...])
    oh = jnp.concatenate(oht, axis=0).T.astype(BF16)
    center = jnp.concatenate([oht[3]] * 3 + [jnp.zeros_like(oht[3])] * 5, axis=0).T.astype(BF16)
    keys = [jnp.concatenate([oh, oh, oh, counts(center, backward)], axis=1) for backward in (False, True)]
    center = center[:, :24]

    lane = lax.broadcasted_iota(jnp.int32, (CH, SB), 1)
    row = lax.broadcasted_iota(jnp.int32, (CH, SB), 0)
    within = lane % CH
    diag = within == row
    low = lane < CH
    neg = (
        jnp.where(within <= row, 0.0, -1e30).astype(F32),
        jnp.where(within >= row, 0.0, -1e30).astype(F32),
    )
    lane8 = lax.broadcasted_iota(jnp.int32, (8, SB), 1)
    row8 = lax.broadcasted_iota(jnp.int32, (8, SB), 0)
    rolled = pltpu.roll(oht[3], CH, 1)
    ot2 = (jnp.where(lane8 < CH, oht[3], rolled), jnp.where(lane8 < CH, rolled, oht[3]))

    scores = []
    for strand in range(2):
        per_chunk = []
        for c in range(2):
            acc = None
            for b in range(5):
                term = s_ref[strand, b] * ot2[c][b : b + 1, :]
                acc = term if acc is None else acc + term
            per_chunk.append(dot(center[c * CH : (c + 1) * CH], stack3(acc)))
        scores.append(per_chunk)

    for n, (strand, k, backward) in enumerate(CHAINS):
        d = int(backward)
        for pair in range(4):
            cols = slice(n * E + pair * SB, n * E + (pair + 1) * SB)
            base = (n * 4 + pair) * 3 * SB
            found = dot(keys[d], tab_ref[:, base : base + 3 * SB])
            pre = found[:, :SB]
            xc = pre * jax.nn.sigmoid(pre)
            xw = xc * found[:, SB : 2 * SB]
            cum = found[:, 2 * SB :]
            xh = xw.astype(BF16)
            xl = (xw - xh.astype(F32)).astype(BF16)
            for c in range(2):
                rows = slice(c * CH, (c + 1) * CH)
                cc = cum[rows]
                rowv = jnp.sum(jnp.where(diag, cc, 0.0), axis=0, keepdims=True)
                last = cc[0:1, :] if backward else cc[CH - 1 : CH, :]
                m = jnp.exp2(jnp.minimum(cc - rowv, neg[d])) * scores[strand][c]
                ext = jnp.exp2(jnp.minimum(last - rowv, 0.0)) * ot2[c]
                full = jnp.concatenate([m, ext, jnp.zeros_like(ext)], axis=0)
                mh = full.astype(BF16)
                ml = (full - mh.astype(F32)).astype(BF16)
                lhs = jnp.concatenate([mh, ml], axis=1)
                zero = jnp.zeros((CH, SB), BF16)
                top = jnp.concatenate([jnp.where(low, xh[rows], zero), jnp.where(low, xl[rows], zero)], axis=1)
                bot = jnp.concatenate([jnp.where(low, zero, xh[rows]), jnp.where(low, zero, xl[rows])], axis=1)
                rhs = jnp.concatenate([top, bot, top, bot], axis=0)
                out = dot(lhs, rhs)
                out = out[:, :SB] + out[:, SB:]
                y_ref[rows, cols] = out[:CH] + skip_ref[0:1, cols] * xc[rows]
                u = out[CH : CH + 8]
                ps = slice(pair * SB, (pair + 1) * SB)
                u_ref[c, n, :, ps] = jnp.where(row8 == 5, jnp.broadcast_to(last, (8, SB)), u)
                dacc = dacc_ref[n, 0:1, ps]
                eacc = eacc_ref[n, :, ps]
                if backward:
                    eacc = eacc + jnp.exp2(dacc) * u
                else:
                    eacc = eacc * jnp.exp2(last) + u
                dacc = dacc + last
                dacc_ref[n, 0:1, ps] = dacc
                eacc_ref[n, :, ps] = eacc
                end_ref[n, :, ps] = jnp.where(row8 == 5, jnp.broadcast_to(dacc, (8, SB)), eacc)


def finish_kernel(
    chunks, taps_ref, la_ref, s_ref, gate_ref, gain_ref, emb_ref, wo_ref, u_ref, far_ref, y_ref, out_ref, in_ref,
    rev_ref
):
    step = pl.program_id(0)

    @pl.when(step == 0)
    def _():
        r = lax.broadcasted_iota(jnp.int32, (D, D), 0)
        c = lax.broadcasted_iota(jnp.int32, (D, D), 1)
        rev_ref[...] = dot(wo_ref[...], (r + c == D - 1).astype(BF16)).astype(BF16)
        for n, (strand, k, backward) in enumerate(CHAINS):

            def chunk(i, s):
                c = chunks - 1 - i if backward else i
                acc = None
                for b in range(5):
                    col = s_ref[strand, b]
                    term = jnp.concatenate([col] * 4, axis=1) * s[b : b + 1, :]
                    acc = term if acc is None else acc + term
                hi, mid, lo = split3(acc)
                in_ref[c, n] = jnp.concatenate(
                    [hi.astype(F32), mid.astype(F32), lo.astype(F32)], axis=0
                )
                piece = u_ref[c, n]
                return jnp.exp2(piece[5:6, :]) * s + piece

            lax.fori_loop(0, chunks, chunk, far_ref[int(backward), (n % 2) * 8 : (n % 2) * 8 + 8, :])

    center = (
        taps_ref[3:4, :] == lax.broadcasted_iota(jnp.int32, (SB, SB), 0) % 8
    ).astype(F32).T.astype(BF16)[:, :24]
    cnt = (counts(center, False), counts(center, True))
    r = lax.broadcasted_iota(jnp.int32, (2 * SB, SB), 0)
    c = lax.broadcasted_iota(jnp.int32, (2 * SB, SB), 1)
    ones = (((r % SB) // CH) == (c // CH)).astype(BF16)

    total = dot(center[:, :5], emb_ref[...])
    for strand in range(2):
        mixed = []
        for half in range(2):
            ps = slice(half * 2 * SB, (half + 1) * 2 * SB)
            gate = dot(center, gate_ref[:, strand * E + half * 2 * SB : strand * E + (half + 1) * 2 * SB])
            acc = None
            for k in range(2):
                n = [c[:2] for c in CHAINS].index((strand, k))
                backward = CHAINS[n][2]
                cols = slice(n * E + half * 2 * SB, n * E + (half + 1) * 2 * SB)
                reach = jnp.exp2(dot(cnt[int(backward)], la_ref[:, cols]))
                far = jnp.concatenate(
                    [
                        dot(center[h * CH : (h + 1) * CH], in_ref[step * 2 + h, n, :, ps].astype(BF16))
                        for h in range(2)
                    ],
                    axis=0,
                )
                g = (y_ref[:, cols] + reach * far) * gate
                sq = g * g
                sh = sq.astype(BF16)
                sl = (sq - sh.astype(F32)).astype(BF16)
                mean = jnp.concatenate(
                    [
                        dot(jnp.concatenate([sh[:, q * SB : (q + 1) * SB], sl[:, q * SB : (q + 1) * SB]], axis=1), ones)
                        for q in range(2)
                    ],
                    axis=1,
                ) * (1.0 / CH)
                normed = g * lax.rsqrt(mean + EPSILON) * gain_ref[k : k + 1, ps]
                acc = normed if acc is None else acc + normed
            mixed.append(acc.astype(BF16))
        strand_out = dot(jnp.concatenate(mixed, axis=1), (rev_ref if strand else wo_ref)[...])
        total = total + strand_out.astype(BF16).astype(F32)
    out_ref[...] = total.astype(BF16)


def greet(peers):
    barrier = pltpu.get_barrier_semaphore()
    for peer in peers:
        pl.semaphore_signal(barrier, inc=1, device_id={"seq": peer}, device_id_type=MESH)
    pl.semaphore_wait(barrier, len(peers))


def tables_kernel(
    count, tok_ref, emb_ref, w_ref, conv_ref, bias_ref, rate_ref, gain_ref, tab_ref, la_ref, gate_ref, s_ref,
    skip_ref, taps_ref, halo_ref, send_sem, recv_sem
):
    me = lax.axis_index("seq")
    up, down = lax.rem(me + 1, count), lax.rem(me + count - 1, count)
    greet((up, down))
    copies = [
        pltpu.make_async_remote_copy(
            src_ref=tok_ref.at[src], dst_ref=halo_ref.at[slot], send_sem=send_sem.at[slot],
            recv_sem=recv_sem.at[slot], device_id={"seq": peer}, device_id_type=MESH,
        )
        for slot, src, peer in ((0, tok_ref.shape[0] - 1, up), (1, 0, down))
    ]
    for copy in copies:
        copy.start()

    sym = lax.broadcasted_iota(jnp.int32, (16, 5), 0)
    col = lax.broadcasted_iota(jnp.int32, (16, 5), 1)
    paired = jnp.where(sym < 8, sym, jnp.where(sym < 12, 11 - sym, sym - 8))
    both = dot((paired == col).astype(BF16), emb_ref[...]).astype(BF16)
    table = lax.dot_general(
        both, w_ref[...], (((1,), (1,)), ((), ())), preferred_element_type=F32
    ).astype(BF16)
    gate = table[:, :E].astype(F32)
    gate = gate * jax.nn.sigmoid(gate)
    values = table[:, E : 2 * E].astype(F32)
    tail = table[:, 2 * E :]
    width = tail.shape[1]

    def pick(first, cols, group):
        r = lax.broadcasted_iota(jnp.int32, (width, cols), 0)
        c = lax.broadcasted_iota(jnp.int32, (width, cols), 1)
        return dot(tail, (r - first == c // group).astype(BF16))

    raw = pick(2 * NS, E, CH)
    b_part, c_part = pick(0, NS, 1), pick(NS, NS, 1)
    for strand in range(2):
        at = slice(strand * 8, strand * 8 + 8)
        gate_ref[:, strand * E : (strand + 1) * E] = stack3(gate[at])
        for b in range(8):
            row = b_part[strand * 8 + b : strand * 8 + b + 1, :]
            s_ref[strand, b] = jnp.broadcast_to(jnp.sum(c_part[at] * row, axis=1, keepdims=True), (8, SB))
    spread = (
        lax.broadcasted_iota(jnp.int32, (H, E), 0) == lax.broadcasted_iota(jnp.int32, (H, E), 1) // CH
    ).astype(BF16)

    def widen(v):
        hi, mid, lo = split3(v)
        return dot(hi, spread) + dot(mid, spread) + dot(lo, spread)

    bias, rate, skip = widen(bias_ref[...]), widen(rate_ref[...]), widen(gain_ref[...])
    for n, (strand, k, backward) in enumerate(CHAINS):
        at = slice(strand * 8, strand * 8 + 8)
        zero = jnp.zeros((8, E), F32)
        parts = []
        for j in range(8):
            tap = (2 * (KW - 1) - j) if backward else j
            parts.append(conv_ref[k, tap : tap + 1, :] * values[at] if 0 <= tap < KW else zero)
        conv = stack3(jnp.concatenate(parts, axis=0))
        dt = jax.nn.softplus(raw[at] + bias[k : k + 1, :])
        steps = []
        for part in split3(dt):
            steps += [zero] * 3 + [part.astype(F32)] + [zero] * 4
        steps = jnp.concatenate(steps, axis=0).astype(BF16)
        la = [part.astype(F32) for part in split3(-rate[k : k + 1, :] * dt * LOG2E)]
        la_ref[:, n * E : (n + 1) * E] = jnp.concatenate(la, axis=0).astype(BF16)
        la = jnp.concatenate(la + [zero] * 5, axis=0).astype(BF16)
        for pair in range(4):
            ps = slice(pair * SB, (pair + 1) * SB)
            base = (n * 4 + pair) * 3 * SB
            tab_ref[0:192, base : base + SB] = conv[:, ps]
            tab_ref[0:192, base + SB : base + 2 * SB] = steps[:, ps]
            tab_ref[0:192, base + 2 * SB : base + 3 * SB] = jnp.zeros((192, SB), BF16)
            tab_ref[192:256, base : base + 2 * SB] = jnp.zeros((64, 2 * SB), BF16)
            tab_ref[192:256, base + 2 * SB : base + 3 * SB] = la[:, ps]
        skip_ref[:, n * E : (n + 1) * E] = skip[k : k + 1, :]

    for copy in copies:
        copy.wait()
    blocks = tok_ref.shape[0]
    lane = lax.broadcasted_iota(jnp.int32, (8, SB), 1)
    row = lax.broadcasted_iota(jnp.int32, (8, SB), 0)
    rows = [jnp.where(me > 0, halo_ref[0], -1)] + [tok_ref[b] for b in range(blocks)]
    rows.append(jnp.where(me < count - 1, halo_ref[1], -1))
    rows = [jnp.broadcast_to(v, (8, SB)) for v in rows]
    for b in range(blocks):
        before, here, after = rows[b : b + 3]
        out = jnp.where(row == KW - 1, here, -1)
        for shift in range(1, KW):
            down_by = jnp.where(lane < shift, pltpu.roll(before, shift, 1), pltpu.roll(here, shift, 1))
            up_by = jnp.where(
                lane >= SB - shift, pltpu.roll(after, SB - shift, 1), pltpu.roll(here, SB - shift, 1)
            )
            out = jnp.where(row == KW - 1 - shift, down_by, out)
            out = jnp.where(row == KW - 1 + shift, up_by, out)
        taps_ref[:, b * SB : (b + 1) * SB] = out


def compose(earlier, later):
    row = lax.broadcasted_iota(jnp.int32, (8, E), 0)
    parts = []
    for i in range(2):
        e, l = earlier[8 * i : 8 * i + 8], later[8 * i : 8 * i + 8]
        parts.append(jnp.where(row == 5, 1.0, jnp.exp2(l[5:6, :])) * e + l)
    return jnp.concatenate(parts, axis=0)


def scan_kernel(
    count, end_ref, in_ref, pair_ref, back_ref, chip_ref, z_ref, line_ref, y_ref, other_ref, send_sem, recv_sem,
    zsend_sem, zrecv_sem, ysend_sem, yrecv_sem
):
    nz, ny = NZ, count // (NZ * CORES)
    me = lax.axis_index("seq")
    core = lax.rem(me, CORES)
    z = lax.rem(me // CORES, nz)
    y = me // (CORES * nz)
    sign = 1 - 2 * core
    pz = z * sign + core * (nz - 1)
    py = y * sign + core * (ny - 1)
    partner = me + sign
    zpeers = [(y * nz + lax.rem(z + d * sign + nz, nz)) * CORES + core for d in range(1, nz)]
    ypeers = [(lax.rem(y + d * sign + ny, ny) * nz + z) * CORES + core for d in range(1, ny)]
    greet([partner] + zpeers + ypeers)

    def remote(src, dst, send, recv, peer):
        return pltpu.make_async_remote_copy(
            src_ref=src, dst_ref=dst, send_sem=send, recv_sem=recv, device_id={"seq": peer}, device_id_type=MESH
        )

    def merge(position, size, slots_ref, mine):
        before = jnp.zeros_like(mine)
        for d in range(size - 1, 0, -1):
            before = jnp.where(d <= position, compose(before, slots_ref[d - 1]), before)
        total = compose(before, mine)
        for d in range(size - 1, 0, -1):
            total = jnp.where(d > position, compose(total, slots_ref[d - 1]), total)
        return before, total

    copy = remote(end_ref.at[1 - core], pair_ref, send_sem.at[0], recv_sem.at[0], partner)
    copy.start()
    copy.wait()
    mine = end_ref[core]
    chip = compose(mine, pair_ref[...])
    chip_ref[...] = chip
    copies = [
        remote(chip_ref, z_ref.at[d], zsend_sem.at[d], zrecv_sem.at[d], peer) for d, peer in enumerate(zpeers)
    ]
    for copy in copies:
        copy.start()
    for copy in copies:
        copy.wait()
    before, line = merge(pz, nz, z_ref, chip)
    line_ref[...] = line
    copies = [
        remote(line_ref, y_ref.at[d], ysend_sem.at[d], yrecv_sem.at[d], peer) for d, peer in enumerate(ypeers)
    ]
    for copy in copies:
        copy.start()
    for copy in copies:
        copy.wait()
    far, _ = merge(py, ny, y_ref, line)
    incoming = compose(far, before)
    other_ref[...] = compose(incoming, mine)
    copy = remote(other_ref, back_ref, send_sem.at[1], recv_sem.at[1], partner)
    copy.start()
    copy.wait()
    in_ref[core] = incoming
    in_ref[1 - core] = back_ref[...]


def per_device(
    token_ids,
    embed_table,
    input_weight_matrix,
    output_weight_matrix,
    conv_weight,
    dt_bias,
    decay_rate,
    skip_gain,
    norm_gain,
):
    rows = token_ids.shape[0]
    count = lax.axis_size("seq")
    blocks = rows // SB
    chunks = rows // CH

    vmem = pl.BlockSpec(memory_space=pltpu.VMEM)
    token_rows = token_ids.reshape(blocks, 1, SB)
    tab, la3, gate3, score, skip, taps = pl.pallas_call(
        functools.partial(tables_kernel, count),
        out_shape=(
            jax.ShapeDtypeStruct((256, 12 * E), BF16),
            jax.ShapeDtypeStruct((24, 4 * E), BF16),
            jax.ShapeDtypeStruct((24, 2 * E), BF16),
            jax.ShapeDtypeStruct((2, 8, 8, SB), F32),
            jax.ShapeDtypeStruct((1, 4 * E), F32),
            jax.ShapeDtypeStruct((8, rows), jnp.int32),
        ),
        in_specs=[vmem] * 7,
        out_specs=(vmem,) * 6,
        scratch_shapes=[
            pltpu.VMEM((2, 1, SB), jnp.int32), pltpu.SemaphoreType.DMA((2,)), pltpu.SemaphoreType.DMA((2,))
        ],
        compiler_params=pltpu.CompilerParams(collective_id=0, has_side_effects=True),
        name="tables",
    )(token_rows, embed_table, input_weight_matrix.T, conv_weight, dt_bias, decay_rate, skip_gain)

    whole = lambda shape: pl.BlockSpec(shape, lambda i: (0,) * len(shape))
    params = pltpu.CompilerParams(vmem_limit_bytes=56 * 1024 * 1024)
    y, u, end = pl.pallas_call(
        local_kernel,
        grid=(blocks,),
        out_shape=(
            jax.ShapeDtypeStruct((rows, 4 * E), F32),
            jax.ShapeDtypeStruct((chunks, 4, 8, E), F32),
            jax.ShapeDtypeStruct((4, 8, E), F32),
        ),
        in_specs=[
            pl.BlockSpec((8, SB), lambda i: (0, i)),
            whole((256, 12 * E)),
            whole((2, 8, 8, SB)),
            whole((1, 4 * E)),
        ],
        out_specs=(
            pl.BlockSpec((SB, 4 * E), lambda i: (i, 0)),
            pl.BlockSpec((2, 4, 8, E), lambda i: (i, 0, 0, 0)),
            whole((4, 8, E)),
        ),
        scratch_shapes=[pltpu.VMEM((4, 8, E), F32), pltpu.VMEM((4, 8, E), F32)],
        compiler_params=params,
        name="local_chunks",
    )(taps, tab, score, skip)

    nz, ny = NZ, count // (NZ * CORES)
    state = pltpu.VMEM((16, E), F32)
    far = pl.pallas_call(
        functools.partial(scan_kernel, count),
        out_shape=jax.ShapeDtypeStruct((2, 16, E), F32),
        in_specs=[vmem],
        out_specs=vmem,
        scratch_shapes=[
            state,
            state,
            state,
            pltpu.VMEM((max(nz - 1, 1), 16, E), F32),
            state,
            pltpu.VMEM((max(ny - 1, 1), 16, E), F32),
            state,
        ]
        + [pltpu.SemaphoreType.DMA((max(m, 1),)) for m in (2, 2, nz - 1, nz - 1, ny - 1, ny - 1)],
        compiler_params=pltpu.CompilerParams(collective_id=1, has_side_effects=True),
        name="state_scan",
    )(end.reshape(2, 16, E))
    return pl.pallas_call(
        functools.partial(finish_kernel, chunks),
        grid=(blocks,),
        out_shape=jax.ShapeDtypeStruct((rows, D), BF16),
        in_specs=[
            pl.BlockSpec((8, SB), lambda i: (0, i)),
            whole((24, 4 * E)),
            whole((2, 8, 8, SB)),
            whole((24, 2 * E)),
            whole((2, E)),
            whole((5, D)),
            whole((E, D)),
            whole((chunks, 4, 8, E)),
            whole((2, 16, E)),
            pl.BlockSpec((SB, 4 * E), lambda i: (i, 0)),
        ],
        out_specs=pl.BlockSpec((SB, D), lambda i: (i, 0)),
        scratch_shapes=[pltpu.VMEM((chunks, 4, 24, E), F32), pltpu.VMEM((E, D), BF16)],
        compiler_params=params,
        name="finish_rows",
    )(taps, la3, score, gate3, norm_gain, embed_table, output_weight_matrix, u, far, y)


def solution(mesh):
    placed = (P(("batch", "seq")), P(), P(), P(), P(), P(), P(), P(), P())
    return jax.shard_map(
        per_device, mesh=mesh, in_specs=placed, out_specs=P(("batch", "seq"), None), check_vma=False
    )
```

```python
import functools

import jax
import jax.numpy as jnp
from jax import lax
from jax.experimental import pallas as pl
from jax.experimental.pallas import tpu as pltpu
from jax.sharding import PartitionSpec as P

D = 256
E = 512
NS = 16
KW = 4
H = 8
CH = 64
SB = 128
EPSILON = 1e-05
LOG2E = 1.4426950408889634
CORES = 2
WIDE = 4
NZ = 8
CHAINS = ((0, 0, False), (1, 1, False), (0, 1, True), (1, 0, True))
MESH = pl.DeviceIdType.MESH
F32 = jnp.float32
BF16 = jnp.bfloat16


def split3(v):
    hi = v.astype(BF16)
    rest = v - hi.astype(F32)
    mid = rest.astype(BF16)
    lo = (rest - mid.astype(F32)).astype(BF16)
    return hi, mid, lo


def stack3(v):
    return jnp.concatenate(split3(v), axis=0)


def dot(a, b):
    return jnp.dot(a, b, preferred_element_type=F32)


def onehots(taps_row):
    sym = lax.broadcasted_iota(jnp.int32, (8, SB), 0)
    return [(taps_row[j : j + 1, :] == sym).astype(F32) for j in range(8)]


def counts(center, backward):
    r = lax.broadcasted_iota(jnp.int32, (SB, SB), 0)
    c = lax.broadcasted_iota(jnp.int32, (SB, SB), 1)
    same = (r // CH) == (c // CH)
    keep = same & ((c >= r) if backward else (c <= r))
    return dot(keep.astype(BF16), center).astype(BF16)


def local_kernel(taps_ref, tab_ref, s_ref, skip_ref, y_ref, u_ref, end_ref, dacc_ref, eacc_ref):
    step = pl.program_id(0)

    @pl.when(step == 0)
    def _():
        dacc_ref[...] = jnp.zeros_like(dacc_ref)
        eacc_ref[...] = jnp.zeros_like(eacc_ref)

    centers, keys, ot2 = [], [[], []], []
    lane8 = lax.broadcasted_iota(jnp.int32, (8, SB), 1)
    row8 = lax.broadcasted_iota(jnp.int32, (8, SB), 0)
    for part in range(WIDE):
        oht = onehots(taps_ref[:, part * SB : (part + 1) * SB])
        oh = jnp.concatenate(oht, axis=0).T.astype(BF16)
        center = jnp.concatenate([oht[3]] * 3 + [jnp.zeros_like(oht[3])] * 5, axis=0).T.astype(BF16)
        for d in range(2):
            keys[d].append(jnp.concatenate([oh, oh, oh, counts(center, d == 1)], axis=1))
        centers += [center[:CH, :24], center[CH:, :24]]
        rolled = pltpu.roll(oht[3], CH, 1)
        ot2 += [jnp.where(lane8 < CH, oht[3], rolled), jnp.where(lane8 < CH, rolled, oht[3])]
    keys = [jnp.concatenate(v, axis=0) for v in keys]

    lane = lax.broadcasted_iota(jnp.int32, (CH, SB), 1)
    row = lax.broadcasted_iota(jnp.int32, (CH, SB), 0)
    within = lane % CH
    diag = within == row
    low = lane < CH
    neg = (
        jnp.where(within <= row, 0.0, -1e30).astype(F32),
        jnp.where(within >= row, 0.0, -1e30).astype(F32),
    )
    scores = []
    for strand in range(2):
        per_chunk = []
        for c in range(2 * WIDE):
            acc = None
            for b in range(5):
                term = s_ref[strand, b] * ot2[c][b : b + 1, :]
                acc = term if acc is None else acc + term
            per_chunk.append(dot(centers[c], stack3(acc)))
        scores.append(per_chunk)

    for n, (strand, k, backward) in enumerate(CHAINS):
        d = int(backward)
        for pair in range(4):
            cols = slice(n * E + pair * SB, n * E + (pair + 1) * SB)
            base = (n * 4 + pair) * 3 * SB
            found = dot(keys[d], tab_ref[:, base : base + 3 * SB])
            pre = found[:, :SB]
            xc = pre * jax.nn.sigmoid(pre)
            xw = xc * found[:, SB : 2 * SB]
            cum = found[:, 2 * SB :]
            xh = xw.astype(BF16)
            xl = (xw - xh.astype(F32)).astype(BF16)
            for c in range(2 * WIDE):
                rows = slice(c * CH, (c + 1) * CH)
                cc = cum[rows]
                rowv = jnp.sum(jnp.where(diag, cc, 0.0), axis=0, keepdims=True)
                last = cc[0:1, :] if backward else cc[CH - 1 : CH, :]
                m = jnp.exp2(jnp.minimum(cc - rowv, neg[d])) * scores[strand][c]
                ext = jnp.exp2(jnp.minimum(last - rowv, 0.0)) * ot2[c]
                full = jnp.concatenate([m, ext, jnp.zeros_like(ext)], axis=0)
                mh = full.astype(BF16)
                ml = (full - mh.astype(F32)).astype(BF16)
                lhs = jnp.concatenate([mh, ml], axis=1)
                zero = jnp.zeros((CH, SB), BF16)
                top = jnp.concatenate([jnp.where(low, xh[rows], zero), jnp.where(low, xl[rows], zero)], axis=1)
                bot = jnp.concatenate([jnp.where(low, zero, xh[rows]), jnp.where(low, zero, xl[rows])], axis=1)
                rhs = jnp.concatenate([top, bot, top, bot], axis=0)
                out = dot(lhs, rhs)
                out = out[:, :SB] + out[:, SB:]
                y_ref[rows, cols] = out[:CH] + skip_ref[0:1, cols] * xc[rows]
                u = out[CH : CH + 8]
                ps = slice(pair * SB, (pair + 1) * SB)
                u_ref[c, n, :, ps] = jnp.where(row8 == 5, jnp.broadcast_to(last, (8, SB)), u)
                dacc = dacc_ref[n, 0:1, ps]
                eacc = eacc_ref[n, :, ps]
                if backward:
                    eacc = eacc + jnp.exp2(dacc) * u
                else:
                    eacc = eacc * jnp.exp2(last) + u
                dacc = dacc + last
                dacc_ref[n, 0:1, ps] = dacc
                eacc_ref[n, :, ps] = eacc
                end_ref[n, :, ps] = jnp.where(row8 == 5, jnp.broadcast_to(dacc, (8, SB)), eacc)


def finish_kernel(
    chunks, taps_ref, la_ref, s_ref, gate_ref, gain_ref, emb_ref, wo_ref, u_ref, far_ref, y_ref, out_ref, in_ref,
    rev_ref
):
    step = pl.program_id(0)

    @pl.when(step == 0)
    def _():
        r = lax.broadcasted_iota(jnp.int32, (D, D), 0)
        c = lax.broadcasted_iota(jnp.int32, (D, D), 1)
        rev_ref[...] = dot(wo_ref[...], (r + c == D - 1).astype(BF16)).astype(BF16)

        def chunk(i, states):
            following = []
            for n, (strand, k, backward) in enumerate(CHAINS):
                c = chunks - 1 - i if backward else i
                s = states[n]
                acc = None
                for b in range(5):
                    col = s_ref[strand, b]
                    term = jnp.concatenate([col] * 4, axis=1) * s[b : b + 1, :]
                    acc = term if acc is None else acc + term
                hi, mid, lo = split3(acc)
                in_ref[c, n] = jnp.concatenate(
                    [hi.astype(F32), mid.astype(F32), lo.astype(F32)], axis=0
                )
                piece = u_ref[c, n]
                following.append(jnp.exp2(piece[5:6, :]) * s + piece)
            return tuple(following)

        start = tuple(far_ref[n // 2, (n % 2) * 8 : (n % 2) * 8 + 8, :] for n in range(4))
        lax.fori_loop(0, chunks, chunk, start, unroll=2)

    center = (
        taps_ref[3:4, :] == lax.broadcasted_iota(jnp.int32, (SB, SB), 0) % 8
    ).astype(F32).T.astype(BF16)[:, :24]
    cnt = (counts(center, False), counts(center, True))
    r = lax.broadcasted_iota(jnp.int32, (2 * SB, SB), 0)
    c = lax.broadcasted_iota(jnp.int32, (2 * SB, SB), 1)
    ones = (((r % SB) // CH) == (c // CH)).astype(BF16)

    upper = lax.broadcasted_iota(jnp.int32, (SB, 24), 0) < CH
    wide = center.astype(F32)
    placed = jnp.concatenate([jnp.where(upper, wide, 0.0), jnp.where(upper, 0.0, wide)], axis=1).astype(BF16)
    total = dot(center[:, :5], emb_ref[...])
    for strand in range(2):
        mixed = []
        for half in range(2):
            ps = slice(half * 2 * SB, (half + 1) * 2 * SB)
            gate = dot(center, gate_ref[:, strand * E + half * 2 * SB : strand * E + (half + 1) * 2 * SB])
            acc = None
            for k in range(2):
                n = [c[:2] for c in CHAINS].index((strand, k))
                backward = CHAINS[n][2]
                cols = slice(n * E + half * 2 * SB, n * E + (half + 1) * 2 * SB)
                reach = jnp.exp2(dot(cnt[int(backward)], la_ref[:, cols]))
                entry = jnp.concatenate([in_ref[step * 2, n, :, ps], in_ref[step * 2 + 1, n, :, ps]], axis=0)
                far = dot(placed, entry.astype(BF16))
                g = (y_ref[:, cols] + reach * far) * gate
                sq = g * g
                sh = sq.astype(BF16)
                sl = (sq - sh.astype(F32)).astype(BF16)
                mean = dot(
                    jnp.concatenate(
                        [
                            jnp.concatenate([v[:, q * SB : (q + 1) * SB] for v in (sh, sl)], axis=1)
                            for q in range(2)
                        ],
                        axis=0,
                    ),
                    ones,
                )
                mean = jnp.concatenate([mean[:SB], mean[SB:]], axis=1) * (1.0 / CH)
                normed = g * lax.rsqrt(mean + EPSILON) * gain_ref[k : k + 1, ps]
                acc = normed if acc is None else acc + normed
            mixed.append(acc.astype(BF16))
        strand_out = dot(jnp.concatenate(mixed, axis=1), (rev_ref if strand else wo_ref)[...])
        total = total + strand_out.astype(BF16).astype(F32)
    out_ref[...] = total.astype(BF16)


def greet(peers):
    barrier = pltpu.get_barrier_semaphore()
    for peer in peers:
        pl.semaphore_signal(barrier, inc=1, device_id={"seq": peer}, device_id_type=MESH)
    pl.semaphore_wait(barrier, len(peers))


def tables_kernel(
    count, tok_ref, emb_ref, w_ref, conv_ref, bias_ref, rate_ref, gain_ref, tab_ref, la_ref, gate_ref, s_ref,
    skip_ref, taps_ref, halo_ref, send_sem, recv_sem
):
    me = lax.axis_index("seq")
    up, down = lax.rem(me + 1, count), lax.rem(me + count - 1, count)
    greet((up, down))
    copies = [
        pltpu.make_async_remote_copy(
            src_ref=tok_ref.at[src], dst_ref=halo_ref.at[slot], send_sem=send_sem.at[slot],
            recv_sem=recv_sem.at[slot], device_id={"seq": peer}, device_id_type=MESH,
        )
        for slot, src, peer in ((0, tok_ref.shape[0] - 1, up), (1, 0, down))
    ]
    for copy in copies:
        copy.start()

    sym = lax.broadcasted_iota(jnp.int32, (16, 5), 0)
    col = lax.broadcasted_iota(jnp.int32, (16, 5), 1)
    paired = jnp.where(sym < 8, sym, jnp.where(sym < 12, 11 - sym, sym - 8))
    both = dot((paired == col).astype(BF16), emb_ref[...]).astype(BF16)
    table = lax.dot_general(
        both, w_ref[...], (((1,), (1,)), ((), ())), preferred_element_type=F32
    ).astype(BF16)
    gate = table[:, :E].astype(F32)
    gate = gate * jax.nn.sigmoid(gate)
    values = table[:, E : 2 * E].astype(F32)
    tail = table[:, 2 * E :]
    width = tail.shape[1]

    def pick(first, cols, group):
        r = lax.broadcasted_iota(jnp.int32, (width, cols), 0)
        c = lax.broadcasted_iota(jnp.int32, (width, cols), 1)
        return dot(tail, (r - first == c // group).astype(BF16))

    raw = pick(2 * NS, E, CH)
    b_part, c_part = pick(0, NS, 1), pick(NS, NS, 1)
    for strand in range(2):
        at = slice(strand * 8, strand * 8 + 8)
        gate_ref[:, strand * E : (strand + 1) * E] = stack3(gate[at])
        for b in range(8):
            row = b_part[strand * 8 + b : strand * 8 + b + 1, :]
            s_ref[strand, b] = jnp.broadcast_to(jnp.sum(c_part[at] * row, axis=1, keepdims=True), (8, SB))
    spread = (
        lax.broadcasted_iota(jnp.int32, (H, E), 0) == lax.broadcasted_iota(jnp.int32, (H, E), 1) // CH
    ).astype(BF16)

    def widen(v):
        hi, mid, lo = split3(v)
        return dot(hi, spread) + dot(mid, spread) + dot(lo, spread)

    bias, rate, skip = widen(bias_ref[...]), widen(rate_ref[...]), widen(gain_ref[...])
    for n, (strand, k, backward) in enumerate(CHAINS):
        at = slice(strand * 8, strand * 8 + 8)
        zero = jnp.zeros((8, E), F32)
        parts = []
        for j in range(8):
            tap = (2 * (KW - 1) - j) if backward else j
            parts.append(conv_ref[k, tap : tap + 1, :] * values[at] if 0 <= tap < KW else zero)
        conv = stack3(jnp.concatenate(parts, axis=0))
        dt = jax.nn.softplus(raw[at] + bias[k : k + 1, :])
        steps = []
        for part in split3(dt):
            steps += [zero] * 3 + [part.astype(F32)] + [zero] * 4
        steps = jnp.concatenate(steps, axis=0).astype(BF16)
        la = [part.astype(F32) for part in split3(-rate[k : k + 1, :] * dt * LOG2E)]
        la_ref[:, n * E : (n + 1) * E] = jnp.concatenate(la, axis=0).astype(BF16)
        la = jnp.concatenate(la + [zero] * 5, axis=0).astype(BF16)
        for pair in range(4):
            ps = slice(pair * SB, (pair + 1) * SB)
            base = (n * 4 + pair) * 3 * SB
            tab_ref[0:192, base : base + SB] = conv[:, ps]
            tab_ref[0:192, base + SB : base + 2 * SB] = steps[:, ps]
            tab_ref[0:192, base + 2 * SB : base + 3 * SB] = jnp.zeros((192, SB), BF16)
            tab_ref[192:256, base : base + 2 * SB] = jnp.zeros((64, 2 * SB), BF16)
            tab_ref[192:256, base + 2 * SB : base + 3 * SB] = la[:, ps]
        skip_ref[:, n * E : (n + 1) * E] = skip[k : k + 1, :]

    for copy in copies:
        copy.wait()
    blocks = tok_ref.shape[0]
    lane = lax.broadcasted_iota(jnp.int32, (8, SB), 1)
    row = lax.broadcasted_iota(jnp.int32, (8, SB), 0)
    rows = [jnp.where(me > 0, halo_ref[0], -1)] + [tok_ref[b] for b in range(blocks)]
    rows.append(jnp.where(me < count - 1, halo_ref[1], -1))
    rows = [jnp.broadcast_to(v, (8, SB)) for v in rows]
    for b in range(blocks):
        before, here, after = rows[b : b + 3]
        out = jnp.where(row == KW - 1, here, -1)
        for shift in range(1, KW):
            down_by = jnp.where(lane < shift, pltpu.roll(before, shift, 1), pltpu.roll(here, shift, 1))
            up_by = jnp.where(
                lane >= SB - shift, pltpu.roll(after, SB - shift, 1), pltpu.roll(here, SB - shift, 1)
            )
            out = jnp.where(row == KW - 1 - shift, down_by, out)
            out = jnp.where(row == KW - 1 + shift, up_by, out)
        taps_ref[:, b * SB : (b + 1) * SB] = out


def compose(earlier, later):
    row = lax.broadcasted_iota(jnp.int32, (8, E), 0)
    parts = []
    for i in range(2):
        e, l = earlier[8 * i : 8 * i + 8], later[8 * i : 8 * i + 8]
        parts.append(jnp.where(row == 5, 1.0, jnp.exp2(l[5:6, :])) * e + l)
    return jnp.concatenate(parts, axis=0)


def scan_kernel(
    count, end_ref, in_ref, pair_ref, back_ref, chip_ref, z_ref, line_ref, y_ref, other_ref, send_sem, recv_sem,
    zsend_sem, zrecv_sem, ysend_sem, yrecv_sem
):
    nz, ny = NZ, count // (NZ * CORES)
    me = lax.axis_index("seq")
    core = lax.rem(me, CORES)
    z = lax.rem(me // CORES, nz)
    y = me // (CORES * nz)
    sign = 1 - 2 * core
    pz = z * sign + core * (nz - 1)
    py = y * sign + core * (ny - 1)
    partner = me + sign
    zpeers = [(y * nz + lax.rem(z + d * sign + nz, nz)) * CORES + core for d in range(1, nz)]
    ypeers = [(lax.rem(y + d * sign + ny, ny) * nz + z) * CORES + core for d in range(1, ny)]
    greet([partner] + zpeers + ypeers)

    def remote(src, dst, send, recv, peer):
        return pltpu.make_async_remote_copy(
            src_ref=src, dst_ref=dst, send_sem=send, recv_sem=recv, device_id={"seq": peer}, device_id_type=MESH
        )

    def merge(position, size, slots_ref, mine):
        before = jnp.zeros_like(mine)
        for d in range(size - 1, 0, -1):
            before = jnp.where(d <= position, compose(before, slots_ref[d - 1]), before)
        total = compose(before, mine)
        for d in range(size - 1, 0, -1):
            total = jnp.where(d > position, compose(total, slots_ref[d - 1]), total)
        return before, total

    copy = remote(end_ref.at[1 - core], pair_ref, send_sem.at[0], recv_sem.at[0], partner)
    copy.start()
    copy.wait()
    mine = end_ref[core]
    chip = compose(mine, pair_ref[...])
    chip_ref[...] = chip
    copies = [
        remote(chip_ref, z_ref.at[d], zsend_sem.at[d], zrecv_sem.at[d], peer) for d, peer in enumerate(zpeers)
    ]
    for copy in copies:
        copy.start()
    for copy in copies:
        copy.wait()
    before, line = merge(pz, nz, z_ref, chip)
    line_ref[...] = line
    copies = [
        remote(line_ref, y_ref.at[d], ysend_sem.at[d], yrecv_sem.at[d], peer) for d, peer in enumerate(ypeers)
    ]
    for copy in copies:
        copy.start()
    for copy in copies:
        copy.wait()
    far, _ = merge(py, ny, y_ref, line)
    incoming = compose(far, before)
    other_ref[...] = compose(incoming, mine)
    copy = remote(other_ref, back_ref, send_sem.at[1], recv_sem.at[1], partner)
    copy.start()
    copy.wait()
    in_ref[core] = incoming
    in_ref[1 - core] = back_ref[...]


def per_device(
    token_ids,
    embed_table,
    input_weight_matrix,
    output_weight_matrix,
    conv_weight,
    dt_bias,
    decay_rate,
    skip_gain,
    norm_gain,
):
    rows = token_ids.shape[0]
    count = lax.axis_size("seq")
    blocks = rows // SB
    chunks = rows // CH

    vmem = pl.BlockSpec(memory_space=pltpu.VMEM)
    token_rows = token_ids.reshape(blocks, 1, SB)
    tab, la3, gate3, score, skip, taps = pl.pallas_call(
        functools.partial(tables_kernel, count),
        out_shape=(
            jax.ShapeDtypeStruct((256, 12 * E), BF16),
            jax.ShapeDtypeStruct((24, 4 * E), BF16),
            jax.ShapeDtypeStruct((24, 2 * E), BF16),
            jax.ShapeDtypeStruct((2, 8, 8, SB), F32),
            jax.ShapeDtypeStruct((1, 4 * E), F32),
            jax.ShapeDtypeStruct((8, rows), jnp.int32),
        ),
        in_specs=[vmem] * 7,
        out_specs=(vmem,) * 6,
        scratch_shapes=[
            pltpu.VMEM((2, 1, SB), jnp.int32), pltpu.SemaphoreType.DMA((2,)), pltpu.SemaphoreType.DMA((2,))
        ],
        compiler_params=pltpu.CompilerParams(collective_id=0, has_side_effects=True),
        name="tables",
    )(token_rows, embed_table, input_weight_matrix.T, conv_weight, dt_bias, decay_rate, skip_gain)

    whole = lambda shape: pl.BlockSpec(shape, lambda i: (0,) * len(shape))
    params = pltpu.CompilerParams(vmem_limit_bytes=56 * 1024 * 1024)
    y, u, end = pl.pallas_call(
        local_kernel,
        grid=(blocks // WIDE,),
        out_shape=(
            jax.ShapeDtypeStruct((rows, 4 * E), F32),
            jax.ShapeDtypeStruct((chunks, 4, 8, E), F32),
            jax.ShapeDtypeStruct((4, 8, E), F32),
        ),
        in_specs=[
            pl.BlockSpec((8, WIDE * SB), lambda i: (0, i)),
            whole((256, 12 * E)),
            whole((2, 8, 8, SB)),
            whole((1, 4 * E)),
        ],
        out_specs=(
            pl.BlockSpec((WIDE * SB, 4 * E), lambda i: (i, 0)),
            pl.BlockSpec((2 * WIDE, 4, 8, E), lambda i: (i, 0, 0, 0)),
            whole((4, 8, E)),
        ),
        scratch_shapes=[pltpu.VMEM((4, 8, E), F32), pltpu.VMEM((4, 8, E), F32)],
        compiler_params=params,
        name="local_chunks",
    )(taps, tab, score, skip)

    nz, ny = NZ, count // (NZ * CORES)
    state = pltpu.VMEM((16, E), F32)
    far = pl.pallas_call(
        functools.partial(scan_kernel, count),
        out_shape=jax.ShapeDtypeStruct((2, 16, E), F32),
        in_specs=[vmem],
        out_specs=vmem,
        scratch_shapes=[
            state,
            state,
            state,
            pltpu.VMEM((max(nz - 1, 1), 16, E), F32),
            state,
            pltpu.VMEM((max(ny - 1, 1), 16, E), F32),
            state,
        ]
        + [pltpu.SemaphoreType.DMA((max(m, 1),)) for m in (2, 2, nz - 1, nz - 1, ny - 1, ny - 1)],
        compiler_params=pltpu.CompilerParams(collective_id=1, has_side_effects=True),
        name="state_scan",
    )(end.reshape(2, 16, E))
    return pl.pallas_call(
        functools.partial(finish_kernel, chunks),
        grid=(blocks,),
        out_shape=jax.ShapeDtypeStruct((rows, D), BF16),
        in_specs=[
            pl.BlockSpec((8, SB), lambda i: (0, i)),
            whole((24, 4 * E)),
            whole((2, 8, 8, SB)),
            whole((24, 2 * E)),
            whole((2, E)),
            whole((5, D)),
            whole((E, D)),
            whole((chunks, 4, 8, E)),
            whole((2, 16, E)),
            pl.BlockSpec((SB, 4 * E), lambda i: (i, 0)),
        ],
        out_specs=pl.BlockSpec((SB, D), lambda i: (i, 0)),
        scratch_shapes=[pltpu.VMEM((chunks, 4, 24, E), F32), pltpu.VMEM((E, D), BF16)],
        compiler_params=params,
        name="finish_rows",
    )(taps, la3, score, gate3, norm_gain, embed_table, output_weight_matrix, u, far, y)


def solution(mesh):
    placed = (P(("batch", "seq")), P(), P(), P(), P(), P(), P(), P(), P())
    return jax.shard_map(
        per_device, mesh=mesh, in_specs=placed, out_specs=P(("batch", "seq"), None), check_vma=False
    )
```
